32 devices in a mesh: seq: 4 (over x, core), head: 4 (over z), rep: 2 (over y).
Axes of the slice: x: 2, y: 2, z: 4, core: 2. Of those that a mesh axis runs over, the one named last changes fastest.
Arguments:
- queries: bfloat16 [8, 512, 3072], P(('seq', 'rep'), 'head'), may hold values from -18 to 18, as said below
- keys: bfloat16 [8, 512, 3072], P(('seq', 'rep'), 'head'), may hold values from -18 to 18, as said below
- values: bfloat16 [8, 512, 3072], P(('seq', 'rep'), 'head'), may hold values from -6 to 6
- text_kv: bfloat16 [8, 384, 6144], P(('seq', 'rep'), 'head'), may hold values from -18 to 18, as said below
- cotangent: bfloat16 [8, 512, 3072], P(('seq', 'rep'), None, 'head'), may hold values from -6 to 6
Outputs:
- attended: bfloat16 [8, 512, 3072], P(('seq', 'rep'), None, 'head')
- text_grad: bfloat16 [8, 384, 6144], P(('seq', 'rep'), 'head')
The draws below stay inside these ranges and needn't reach their ends.
Inputs may be any that keep to these rules, and one draw needn't show every extreme that they name: `queries`: normal-like entries of order one. `keys`: normal-like entries of order one. `text_kv`: normal-like entries of order one.
All inputs are finite; a program needn't handle non-finite values.
Results may differ from the reference program's by a relative error of at most 0.007.
Values may be sent and summed in bfloat16 or wider, within the bound.
No kernel may reach another device: no remote copies, remote signals or barrier semaphores. Data moves between devices by JAX's collectives and lax.ppermute only.
A program may use at most 64 MiB of HBM per device.

```python
import jax
import jax.numpy as jnp
from jax import lax

HEADS = 24
HD = 128
TXT = 384
L = 512
CLIPS = 8


def draw_queries(key, part):
    drawn = jax.random.truncated_normal(jax.random.fold_in(key, 1), -4.0, 4.0, (CLIPS, L, HEADS * HD), jnp.float32)
    return drawn.astype(jnp.bfloat16)


def draw_keys(key, part):
    drawn = jax.random.truncated_normal(jax.random.fold_in(key, 2), -4.0, 4.0, (CLIPS, L, HEADS * HD), jnp.float32)
    return drawn.astype(jnp.bfloat16)


def draw_text_kv(key, part):
    drawn = jax.random.truncated_normal(jax.random.fold_in(key, 3), -4.0, 4.0, (CLIPS, TXT, HEADS, 2, HD), jnp.float32)
    return drawn.reshape(CLIPS, TXT, HEADS * 2 * HD).astype(jnp.bfloat16)


def level_of(stream_key, extent, shards, smallest, high):
    loudness = 1.0
    for axis_at, blocks in shards:
        draws = jax.random.uniform(jax.random.fold_in(jax.random.fold_in(stream_key, 6), axis_at), (blocks,), jnp.float32, smallest / len(shards), high / len(shards))
        loudness = loudness * jnp.repeat(jnp.exp(draws), extent[axis_at] // blocks).reshape((-1,) + (1,) * (len(extent) - 1 - axis_at))
    return loudness


def noise(key, extent, spread, most, cuts=(), kind=jnp.bfloat16):
    gain = level_of(key, extent, cuts, -0.22, 0.18) if cuts else 1.0
    result = jax.random.normal(key, extent, jnp.float32) * spread * gain
    return jnp.minimum(jnp.maximum(result, -most), most).astype(kind)


def setup_inputs(seed: int = 0) -> dict:
    key_list = jax.random.split(jax.random.key(seed), 6)
    queries = draw_queries(jax.random.fold_in(key_list[5], 71), 0)
    keys = draw_keys(jax.random.fold_in(key_list[5], 71), 0)
    values = noise(key_list[2], (CLIPS, L, HEADS * HD), 1.0, 6.0, ((0, 8), (1, 4)))
    text_kv = draw_text_kv(jax.random.fold_in(key_list[5], 71), 0)
    cotangent = noise(key_list[4], (CLIPS, L, HEADS * HD), 1.0, 6.0, ((0, 8), (2, 4)))
    return {"queries": queries, "keys": keys, "values": values, "text_kv": text_kv, "cotangent": cotangent}


def softmax_rows(scores):
    top = jnp.max(scores, axis=-1, keepdims=True)
    weights = jnp.exp(scores - top)
    return weights / jnp.sum(weights, axis=-1, keepdims=True)


def block_rows(total):
    return 512 if total % 512 == 0 else total


def attend_block(query_block, grad_block, key_all, value_all, text_keys, text_values, scale):
    query_f = query_block.astype(jnp.float32)
    grad_f = grad_block.astype(jnp.float32)
    scores = jnp.einsum("bgd,lgd->gbl", query_f, key_all.astype(jnp.float32)) * scale
    probs = softmax_rows(scores).astype(jnp.bfloat16)
    self_out = jnp.einsum("gbl,lgd->bgd", probs.astype(jnp.float32), value_all.astype(jnp.float32))
    text_keys_f = text_keys.astype(jnp.float32)
    text_values_f = text_values.astype(jnp.float32)
    cross_scores = jnp.einsum("bgd,tgd->gbt", query_f, text_keys_f) * scale
    cross_probs = softmax_rows(cross_scores)
    cross_rounded = cross_probs.astype(jnp.bfloat16).astype(jnp.float32)
    cross_out = jnp.einsum("gbt,tgd->bgd", cross_rounded, text_values_f)
    attended = (self_out + cross_out).astype(jnp.bfloat16)
    grad_values = jnp.einsum("gbt,bgd->tgd", cross_rounded, grad_f)
    dprobs = jnp.einsum("bgd,tgd->gbt", grad_f, text_values_f)
    dscores = cross_probs * (dprobs - jnp.sum(dprobs * cross_probs, axis=-1, keepdims=True))
    dscores = dscores.astype(jnp.bfloat16).astype(jnp.float32)
    grad_keys = jnp.einsum("gbt,bgd->tgd", dscores, query_f) * scale
    return attended, grad_keys, grad_values


def reference(queries, keys, values, text_kv, cotangent):
    scale = float(HD) ** -0.5
    block = block_rows(L)
    count_blocks = L // block

    def one_clip(carry, inputs):
        query_clip, key_clip, value_clip, text_clip, grad_clip = inputs
        text_heads = text_clip.reshape(TXT, HEADS, 2, HD)
        text_keys = text_heads[:, :, 0, :]
        text_values = text_heads[:, :, 1, :]
        query_heads = query_clip.reshape(count_blocks, block, HEADS, HD)
        grad_heads = grad_clip.reshape(count_blocks, block, HEADS, HD)
        key_heads = key_clip.reshape(L, HEADS, HD)
        value_heads = value_clip.reshape(L, HEADS, HD)

        def one_block(inner, pieces):
            attended, grad_keys, grad_values = attend_block(pieces[0], pieces[1], key_heads, value_heads, text_keys, text_values, scale)
            return (inner[0] + grad_keys, inner[1] + grad_values), attended

        zeros = jnp.zeros((TXT, HEADS, HD), jnp.float32)
        (grad_keys, grad_values), outputs = lax.scan(one_block, (zeros, zeros), (query_heads, grad_heads))
        grads = jnp.stack([grad_keys, grad_values], axis=2).reshape(TXT, HEADS * 2 * HD).astype(jnp.bfloat16)
        return carry, (outputs.reshape(L, HEADS * HD), grads)

    _, (attended, text_grad) = lax.scan(one_clip, jnp.zeros((), jnp.float32), (queries, keys, values, text_kv, cotangent))
    return attended, text_grad
```

```python
import jax
import jax.numpy as jnp
from jax import lax
from jax.experimental import pallas as pl
from jax.experimental.pallas import tpu as pltpu
from jax.sharding import PartitionSpec as P

HD = 128


def dot_nt(a, b):
    return lax.dot_general(a, b, (((1,), (1,)), ((), ())), preferred_element_type=jnp.float32)


def dot_nn(a, b):
    return lax.dot_general(a, b, (((1,), (0,)), ((), ())), preferred_element_type=jnp.float32)


def softmax_columns(scores):
    top = jnp.max(scores, axis=0, keepdims=True)
    weights = jnp.exp(scores - top)
    return weights / jnp.sum(weights, axis=0, keepdims=True)


def gather_queries(order, query_refs, query_all):
    rows = query_refs[0].shape[0]
    for at, ref in enumerate(query_refs):
        query_all[pl.ds(pl.multiple_of(order[at] * rows, rows), rows), :] = ref[...]


def cross_kernel(count, order, *refs):
    query_refs = refs[:count]
    text_refs = refs[count : 2 * count]
    grad_ref = refs[2 * count]
    out_ref = refs[2 * count + 1]
    piece_refs = refs[2 * count + 2 : 3 * count + 2]
    query_all = refs[3 * count + 2]
    scale = float(HD) ** (-0.5)
    gather_queries(order, query_refs, query_all)
    query = query_all[...]
    grad = grad_ref[...]
    text = jnp.concatenate([ref[...] for ref in text_refs], axis=0)
    text_keys = text[:, :HD]
    text_values = text[:, HD:]
    probs = softmax_columns(dot_nt(text_keys, query) * scale)
    rounded = probs.astype(jnp.bfloat16)
    dprobs = dot_nt(text_values, grad)
    dscores = probs * (dprobs - jnp.sum(dprobs * probs, axis=0, keepdims=True))
    dscores = dscores.astype(jnp.bfloat16)
    grad_keys = (dot_nn(dscores, query) * scale).astype(jnp.bfloat16)
    grad_values = dot_nn(rounded, grad).astype(jnp.bfloat16)
    rows = text_refs[0].shape[0]
    for at, ref in enumerate(piece_refs):
        ref[:, :HD] = grad_keys[at * rows : (at + 1) * rows]
        ref[:, HD:] = grad_values[at * rows : (at + 1) * rows]
    out_ref[...] = dot_nn(text_values.T, rounded).T


def self_kernel(count, order, *refs):
    query_refs = refs[:count]
    key_refs = refs[count : 2 * count]
    value_refs = refs[2 * count : 3 * count]
    cross_ref = refs[3 * count]
    out_ref = refs[3 * count + 1]
    query_all = refs[3 * count + 2]
    scale = float(HD) ** (-0.5)
    gather_queries(order, query_refs, query_all)
    keys = jnp.concatenate([ref[...] for ref in key_refs], axis=0)
    values = jnp.concatenate([ref[...] for ref in value_refs], axis=0).T
    length = query_all.shape[0]
    block = 512 if length % 512 == 0 else length
    for start in range(0, length, block):
        rows = pl.ds(start, block)
        probs = softmax_columns(dot_nt(keys, query_all[rows, :]) * scale).astype(jnp.bfloat16)
        out_ref[rows, :] = (dot_nn(values, probs).T + cross_ref[rows, :]).astype(jnp.bfloat16)


def column_block(rows, width):
    return pl.BlockSpec((rows, width), lambda head, order: (0, head))


def cross_call(order, query_pieces, text_pieces, cotangent):
    count = len(query_pieces)
    length, width = cotangent.shape
    heads = width // HD
    rows = query_pieces[0].shape[0]
    text_rows = text_pieces[0].shape[0]
    piece = jax.ShapeDtypeStruct(text_pieces[0].shape, jnp.bfloat16)
    return pl.pallas_call(
        lambda *refs: cross_kernel(count, *refs),
        name="cross",
        out_shape=[jax.ShapeDtypeStruct((length, width), jnp.float32)] + [piece] * count,
        grid_spec=pltpu.PrefetchScalarGridSpec(
            num_scalar_prefetch=1,
            grid=(heads,),
            in_specs=[column_block(rows, HD)] * count
            + [column_block(text_rows, 2 * HD)] * count
            + [column_block(length, HD)],
            out_specs=[column_block(length, HD)] + [column_block(text_rows, 2 * HD)] * count,
            scratch_shapes=[pltpu.VMEM((length, HD), jnp.bfloat16)],
        ),
    )(order, *query_pieces, *text_pieces, cotangent)


def self_call(order, query_pieces, key_pieces, value_pieces, cross_out):
    count = len(query_pieces)
    length, width = cross_out.shape
    heads = width // HD
    rows = query_pieces[0].shape[0]
    return pl.pallas_call(
        lambda *refs: self_kernel(count, *refs),
        name="self",
        out_shape=jax.ShapeDtypeStruct((length, width), jnp.bfloat16),
        grid_spec=pltpu.PrefetchScalarGridSpec(
            num_scalar_prefetch=1,
            grid=(heads,),
            in_specs=[column_block(rows, HD)] * (3 * count) + [column_block(length, HD)],
            out_specs=column_block(length, HD),
            scratch_shapes=[pltpu.VMEM((length, HD), jnp.bfloat16)],
        ),
    )(order, *query_pieces, *key_pieces, *value_pieces, cross_out)


def place_kernel(count, order, *refs):
    pieces = refs[:count]
    out_ref = refs[count]
    sems = refs[count + 1]
    width = pieces[0].shape[1]
    copies = [
        pltpu.make_async_copy(
            piece,
            out_ref.at[:, pl.ds(pl.multiple_of(order[at] * width, width), width)],
            sems.at[at],
        )
        for at, piece in enumerate(pieces)
    ]
    for copy in copies:
        copy.start()
    for copy in copies:
        copy.wait()


def place_call(order, pieces):
    count = len(pieces)
    rows, width = pieces[0].shape
    return pl.pallas_call(
        lambda *refs: place_kernel(count, *refs),
        name="place",
        out_shape=jax.ShapeDtypeStruct((rows, width * count), pieces[0].dtype),
        grid_spec=pltpu.PrefetchScalarGridSpec(
            num_scalar_prefetch=1,
            grid=(1,),
            in_specs=[pl.BlockSpec(memory_space=pl.ANY)] * count,
            out_specs=pl.BlockSpec(memory_space=pl.ANY),
            scratch_shapes=[pltpu.SemaphoreType.DMA((count,))],
        ),
    )(order, *pieces)


def solution(mesh):
    count = mesh.shape["head"]
    paired = count & (count - 1) == 0

    def target(index, step):
        return index ^ step if paired else (index + step) % count

    def origin(index, step):
        return index ^ step if paired else (index - step) % count

    def exchange(pieces):
        return [pieces[0]] + [
            lax.ppermute(
                pieces[step], "head", [(index, target(index, step)) for index in range(count)]
            )
            for step in range(1, count)
        ]

    def send_columns(array, here):
        rows, width = array.shape
        width //= count
        return exchange(
            [
                lax.dynamic_slice(array, (0, target(here, step) * width), (rows, width))
                for step in range(count)
            ]
        )

    def per_device(queries, keys, values, text_kv, cotangent):
        here = lax.axis_index("head")
        order = jnp.stack([origin(here, step) for step in range(count)]).astype(jnp.int32)
        query_pieces = send_columns(queries[0], here)
        text_pieces = send_columns(text_kv[0], here)
        key_pieces = send_columns(keys[0], here)
        value_pieces = send_columns(values[0], here)
        cross_out, *grad_pieces = cross_call(order, query_pieces, text_pieces, cotangent[0])
        back = [
            grad_pieces[0],
        ] + [
            lax.ppermute(
                grad_pieces[step], "head", [(target(index, step), index) for index in range(count)]
            )
            for step in range(1, count)
        ]
        attended = self_call(order, query_pieces, key_pieces, value_pieces, cross_out)
        goal = jnp.stack([target(here, step) for step in range(count)]).astype(jnp.int32)
        return attended[None], place_call(goal, back)[None]

    placed = (
        P(("seq", "rep"), "head", None),
        P(("seq", "rep"), "head", None),
        P(("seq", "rep"), "head", None),
        P(("seq", "rep"), "head", None),
        P(("seq", "rep"), None, "head"),
    )
    return jax.shard_map(
        per_device,
        mesh=mesh,
        in_specs=placed,
        out_specs=(P(("seq", "rep"), None, "head"), P(("seq", "rep"), "head", None)),
        check_vma=False,
    )
```

```python
import jax
import jax.numpy as jnp
from jax import lax
from jax.experimental import pallas as pl
from jax.experimental.pallas import tpu as pltpu
from jax.sharding import PartitionSpec as P


HD = 128


def dot_nt(a, b):
    return lax.dot_general(a, b, (((1,), (1,)), ((), ())), preferred_element_type=jnp.float32)


def dot_nn(a, b):
    return lax.dot_general(a, b, (((1,), (0,)), ((), ())), preferred_element_type=jnp.float32)


def softmax_columns(scores):
    top = jnp.max(scores, axis=0, keepdims=True)
    weights = jnp.exp(scores - top)
    return weights / jnp.sum(weights, axis=0, keepdims=True)


def gather_queries(order, query_refs, query_all):
    rows = query_refs[0].shape[0]
    for at, ref in enumerate(query_refs):
        query_all[pl.ds(pl.multiple_of(order[at] * rows, rows), rows), :] = ref[...]


def cross_kernel(count, order, *refs):
    query_refs = refs[:count]
    text_refs = refs[count : 2 * count]
    grad_ref = refs[2 * count]
    out_ref = refs[2 * count + 1]
    piece_refs = refs[2 * count + 2 : 3 * count + 2]
    query_all = refs[3 * count + 2]
    scale = float(HD) ** (-0.5)
    gather_queries(order, query_refs, query_all)
    query = query_all[...]
    grad = grad_ref[...]
    text = jnp.concatenate([ref[...] for ref in text_refs], axis=0)
    text_keys = text[:, :HD]
    text_values = text[:, HD:]
    probs = softmax_columns(dot_nt(text_keys, query) * scale)
    rounded = probs.astype(jnp.bfloat16)
    dprobs = dot_nt(text_values, grad)
    dscores = probs * (dprobs - jnp.sum(dprobs * probs, axis=0, keepdims=True))
    dscores = dscores.astype(jnp.bfloat16)
    grad_keys = (dot_nn(dscores, query) * scale).astype(jnp.bfloat16)
    grad_values = dot_nn(rounded, grad).astype(jnp.bfloat16)
    rows = text_refs[0].shape[0]
    for at, ref in enumerate(piece_refs):
        ref[:, :HD] = grad_keys[at * rows : (at + 1) * rows]
        ref[:, HD:] = grad_values[at * rows : (at + 1) * rows]
    out_ref[...] = dot_nn(text_values.T, rounded).T


def self_kernel(count, order, *refs):
    query_refs = refs[:count]
    key_refs = refs[count : 2 * count]
    value_refs = refs[2 * count : 3 * count]
    cross_ref = refs[3 * count]
    out_ref = refs[3 * count + 1]
    query_all = refs[3 * count + 2]
    scale = float(HD) ** (-0.5)
    gather_queries(order, query_refs, query_all)
    keys = jnp.concatenate([ref[...] for ref in key_refs], axis=0)
    values = jnp.concatenate([ref[...] for ref in value_refs], axis=0).T
    length = query_all.shape[0]
    block = 512 if length % 512 == 0 else length
    for start in range(0, length, block):
        rows = pl.ds(start, block)
        probs = softmax_columns(dot_nt(keys, query_all[rows, :]) * scale).astype(jnp.bfloat16)
        out_ref[rows, :] = (dot_nn(values, probs).T + cross_ref[rows, :]).astype(jnp.bfloat16)


def column_block(rows, width):
    return pl.BlockSpec((rows, width), lambda head, order: (0, head))


def cross_call(order, query_pieces, text_pieces, cotangent):
    count = len(query_pieces)
    length, width = cotangent.shape
    heads = width // HD
    rows = query_pieces[0].shape[0]
    text_rows = text_pieces[0].shape[0]
    piece = jax.ShapeDtypeStruct(text_pieces[0].shape, jnp.bfloat16)
    return pl.pallas_call(
        lambda *refs: cross_kernel(count, *refs),
        name="cross",
        out_shape=[jax.ShapeDtypeStruct((length, width), jnp.float32)] + [piece] * count,
        grid_spec=pltpu.PrefetchScalarGridSpec(
            num_scalar_prefetch=1,
            grid=(heads,),
            in_specs=[column_block(rows, HD)] * count
            + [column_block(text_rows, 2 * HD)] * count
            + [column_block(length, HD)],
            out_specs=[column_block(length, HD)] + [column_block(text_rows, 2 * HD)] * count,
            scratch_shapes=[pltpu.VMEM((length, HD), jnp.bfloat16)],
        ),
    )(order, *query_pieces, *text_pieces, cotangent)


def self_call(order, query_pieces, key_pieces, value_pieces, cross_out):
    count = len(query_pieces)
    length, width = cross_out.shape
    heads = width // HD
    rows = query_pieces[0].shape[0]
    return pl.pallas_call(
        lambda *refs: self_kernel(count, *refs),
        name="self",
        out_shape=jax.ShapeDtypeStruct((length, width), jnp.bfloat16),
        grid_spec=pltpu.PrefetchScalarGridSpec(
            num_scalar_prefetch=1,
            grid=(heads,),
            in_specs=[column_block(rows, HD)] * (3 * count) + [column_block(length, HD)],
            out_specs=column_block(length, HD),
            scratch_shapes=[pltpu.VMEM((length, HD), jnp.bfloat16)],
        ),
    )(order, *query_pieces, *key_pieces, *value_pieces, cross_out)


def place_kernel(count, order, *refs):
    pieces = refs[:count]
    out_ref = refs[count]
    sems = refs[count + 1]
    width = pieces[0].shape[1]
    copies = [
        pltpu.make_async_copy(
            piece,
            out_ref.at[:, pl.ds(pl.multiple_of(order[at] * width, width), width)],
            sems.at[at],
        )
        for at, piece in enumerate(pieces)
    ]
    for copy in copies:
        copy.start()
    for copy in copies:
        copy.wait()


def place_call(order, pieces):
    count = len(pieces)
    rows, width = pieces[0].shape
    return pl.pallas_call(
        lambda *refs: place_kernel(count, *refs),
        name="place",
        out_shape=jax.ShapeDtypeStruct((rows, width * count), pieces[0].dtype),
        in_specs=[pl.BlockSpec(memory_space=pltpu.SMEM)]
        + [pl.BlockSpec(memory_space=pltpu.VMEM)] * count,
        out_specs=pl.BlockSpec(memory_space=pl.ANY),
        scratch_shapes=[pltpu.SemaphoreType.DMA((count,))],
    )(order, *[pltpu.with_memory_space_constraint(piece, pltpu.VMEM) for piece in pieces])


def send_order(count):
    near, far = [1], list(range(count - 1, 1, -1))
    first = [(name, step) for step in far[:1] for name in ("query", "text")]
    first += [(name, step) for step in near for name in ("query", "text", "key", "value")]
    later = [(name, step) for name in ("query", "text") for step in far[1:]]
    later += [(name, step) for name in ("key", "value") for step in far]
    return first + later


def solution(mesh):
    count = mesh.shape["head"]
    paired = count & (count - 1) == 0

    def target(index, step):
        return index ^ step if paired else (index + step) % count

    def origin(index, step):
        return index ^ step if paired else (index - step) % count

    def per_device(queries, keys, values, text_kv, cotangent):
        here = lax.axis_index("head")
        order = jnp.stack([origin(here, step) for step in range(count)]).astype(jnp.int32)
        goal = jnp.stack([target(here, step) for step in range(count)]).astype(jnp.int32)
        arrays = {"query": queries[0], "text": text_kv[0], "key": keys[0], "value": values[0]}

        def columns(name, step):
            rows, width = arrays[name].shape
            width //= count
            at = target(here, step) * width
            return lax.dynamic_slice(arrays[name], (0, at), (rows, width))

        got = {name: [columns(name, 0)] + [None] * (count - 1) for name in arrays}
        for name, step in sends:
            got[name][step] = lax.ppermute(
                columns(name, step),
                "head",
                [(index, target(index, step)) for index in range(count)],
            )
        cross_out, *grad_pieces = cross_call(order, got["query"], got["text"], cotangent[0])
        back = [grad_pieces[0]]
        for step in range(1, count):
            back.append(
                lax.ppermute(
                    grad_pieces[step],
                    "head",
                    [(target(index, step), index) for index in range(count)],
                )
            )
        attended = self_call(order, got["query"], got["key"], got["value"], cross_out)
        text_grad = place_call(goal, back)
        return attended[None], text_grad[None]

    sends = send_order(count)

    placed = (
        P(("seq", "rep"), "head", None),
        P(("seq", "rep"), "head", None),
        P(("seq", "rep"), "head", None),
        P(("seq", "rep"), "head", None),
        P(("seq", "rep"), None, "head"),
    )
    return jax.shard_map(
        per_device,
        mesh=mesh,
        in_specs=placed,
        out_specs=(P(("seq", "rep"), None, "head"), P(("seq", "rep"), "head", None)),
        check_vma=False,
    )
```

```python
import jax
import jax.numpy as jnp
from jax import lax
from jax.experimental import pallas as pl
from jax.experimental.pallas import tpu as pltpu
from jax.sharding import PartitionSpec as P


HD = 128


def dot_nt(a, b):
    return lax.dot_general(a, b, (((1,), (1,)), ((), ())), preferred_element_type=jnp.float32)


def dot_nn(a, b):
    return lax.dot_general(a, b, (((1,), (0,)), ((), ())), preferred_element_type=jnp.float32)


def softmax_columns(scores):
    top = jnp.max(scores, axis=0, keepdims=True)
    weights = jnp.exp(scores - top)
    return weights / jnp.sum(weights, axis=0, keepdims=True)


def gather_queries(order, query_refs, query_all):
    rows = query_refs[0].shape[0]
    for at, ref in enumerate(query_refs):
        query_all[pl.ds(pl.multiple_of(order[at] * rows, rows), rows), :] = ref[...]


def cross_kernel(count, order, *refs):
    query_refs = refs[:count]
    text_refs = refs[count : 2 * count]
    grad_ref = refs[2 * count]
    out_ref = refs[2 * count + 1]
    piece_refs = refs[2 * count + 2 : 3 * count + 2]
    query_all = refs[3 * count + 2]
    scale = float(HD) ** (-0.5)
    gather_queries(order, query_refs, query_all)
    query = query_all[...]
    grad = grad_ref[...]
    text = jnp.concatenate([ref[...] for ref in text_refs], axis=0)
    text_keys = text[:, :HD]
    text_values = text[:, HD:]
    probs = softmax_columns(dot_nt(text_keys, query) * scale)
    rounded = probs.astype(jnp.bfloat16)
    dprobs = dot_nt(text_values, grad)
    dscores = probs * (dprobs - jnp.sum(dprobs * probs, axis=0, keepdims=True))
    dscores = dscores.astype(jnp.bfloat16)
    grad_keys = (dot_nn(dscores, query) * scale).astype(jnp.bfloat16)
    grad_values = dot_nn(rounded, grad).astype(jnp.bfloat16)
    rows = text_refs[0].shape[0]
    for at, ref in enumerate(piece_refs):
        ref[:, :HD] = grad_keys[at * rows : (at + 1) * rows]
        ref[:, HD:] = grad_values[at * rows : (at + 1) * rows]
    out_ref[...] = dot_nn(text_values.T, rounded).T


def scores_kernel(count, order, *refs):
    query_refs = refs[:count]
    key_refs = refs[count : 2 * count]
    probs_ref = refs[2 * count]
    scale = float(HD) ** (-0.5)
    keys = jnp.concatenate([ref[...] for ref in key_refs], axis=0)
    rows = query_refs[0].shape[0]
    for at, ref in enumerate(query_refs):
        scores = dot_nt(ref[...], keys) * scale
        weights = jnp.exp(scores - jnp.max(scores, axis=1, keepdims=True))
        probs = weights / jnp.sum(weights, axis=1, keepdims=True)
        start = pl.multiple_of(order[at] * rows, rows)
        probs_ref[pl.ds(start, rows), :] = probs.astype(jnp.bfloat16)


def values_kernel(count, *refs):
    value_refs = refs[:count]
    probs_ref, cross_ref, out_ref = refs[count:]
    values = jnp.concatenate([ref[...] for ref in value_refs], axis=0)
    out = dot_nn(probs_ref[...], values)
    out_ref[...] = (out + cross_ref[...]).astype(jnp.bfloat16)


def column_block(rows, width):
    return pl.BlockSpec((rows, width), lambda head, order: (0, head))


def cross_call(order, query_pieces, text_pieces, cotangent):
    count = len(query_pieces)
    length, width = cotangent.shape
    heads = width // HD
    rows = query_pieces[0].shape[0]
    text_rows = text_pieces[0].shape[0]
    piece = jax.ShapeDtypeStruct(text_pieces[0].shape, jnp.bfloat16)
    return pl.pallas_call(
        lambda *refs: cross_kernel(count, *refs),
        name="cross",
        out_shape=[jax.ShapeDtypeStruct((length, width), jnp.float32)] + [piece] * count,
        grid_spec=pltpu.PrefetchScalarGridSpec(
            num_scalar_prefetch=1,
            grid=(heads,),
            in_specs=[column_block(rows, HD)] * count
            + [column_block(text_rows, 2 * HD)] * count
            + [column_block(length, HD)],
            out_specs=[column_block(length, HD)] + [column_block(text_rows, 2 * HD)] * count,
            scratch_shapes=[pltpu.VMEM((length, HD), jnp.bfloat16)],
        ),
    )(order, *query_pieces, *text_pieces, cotangent)


def scores_call(order, query_pieces, key_pieces):
    count = len(query_pieces)
    rows, width = query_pieces[0].shape
    length = rows * count
    heads = width // HD
    return pl.pallas_call(
        lambda *refs: scores_kernel(count, *refs),
        name="scores",
        out_shape=jax.ShapeDtypeStruct((length, heads * length), jnp.bfloat16),
        grid_spec=pltpu.PrefetchScalarGridSpec(
            num_scalar_prefetch=1,
            grid=(heads,),
            in_specs=[column_block(rows, HD)] * (2 * count),
            out_specs=column_block(length, length),
        ),
    )(order, *query_pieces, *key_pieces)


def values_call(value_pieces, probs, cross_out):
    count = len(value_pieces)
    length, width = cross_out.shape
    rows = value_pieces[0].shape[0]
    heads = width // HD

    def block(rows, width):
        return pl.BlockSpec((rows, width), lambda head: (0, head))

    return pl.pallas_call(
        lambda *refs: values_kernel(count, *refs),
        name="values",
        out_shape=jax.ShapeDtypeStruct((length, width), jnp.bfloat16),
        grid=(heads,),
        in_specs=[block(rows, HD)] * count + [block(length, length), block(length, HD)],
        out_specs=block(length, HD),
    )(*value_pieces, probs, cross_out)


def place_kernel(steps, order, *refs):
    pieces = refs[: len(steps)]
    out_ref, sems = refs[-2:]
    width = pieces[0].shape[1]
    copies = [
        pltpu.make_async_copy(
            piece,
            out_ref.at[:, pl.ds(pl.multiple_of(order[step] * width, width), width)],
            sems.at[at],
        )
        for at, (step, piece) in enumerate(zip(steps, pieces))
    ]
    for copy in copies:
        copy.start()
    for copy in copies:
        copy.wait()


def place_call(order, steps, pieces, whole=None):
    count = order.shape[0]
    rows, width = pieces[0].shape
    held = [] if whole is None else [whole]
    return pl.pallas_call(
        lambda *refs: place_kernel(steps, *refs),
        name="place",
        out_shape=jax.ShapeDtypeStruct((rows, width * count), pieces[0].dtype),
        in_specs=[pl.BlockSpec(memory_space=pltpu.SMEM)]
        + [pl.BlockSpec(memory_space=pltpu.VMEM)] * len(steps)
        + [pl.BlockSpec(memory_space=pl.ANY)] * len(held),
        out_specs=pl.BlockSpec(memory_space=pl.ANY),
        scratch_shapes=[pltpu.SemaphoreType.DMA((len(steps),))],
        input_output_aliases={len(steps) + 1: 0} if held else {},
    )(
        order,
        *[pltpu.with_memory_space_constraint(piece, pltpu.VMEM) for piece in pieces],
        *held,
    )


def pick_call(array, at, width):
    def pick_kernel(at, array_ref, out_ref, sem):
        start = pl.multiple_of(at[0] * width, width)
        copy = pltpu.make_async_copy(array_ref.at[:, pl.ds(start, width)], out_ref, sem)
        copy.start()
        copy.wait()

    return pl.pallas_call(
        pick_kernel,
        name="pick",
        out_shape=pltpu.VMEM((array.shape[0], width), array.dtype),
        in_specs=[pl.BlockSpec(memory_space=pltpu.SMEM), pl.BlockSpec(memory_space=pl.ANY)],
        out_specs=pl.BlockSpec(memory_space=pltpu.VMEM),
        scratch_shapes=[pltpu.SemaphoreType.DMA],
    )(at.reshape(1).astype(jnp.int32), array)


def send_order(count):
    near, far = [1], list(range(count - 1, 1, -1))
    first = [(name, step) for step in far[:1] for name in ("query", "text")]
    first += [(name, step) for step in near for name in ("query", "text", "key", "value")]
    later = [(name, step) for name in ("query", "text") for step in far[1:]]
    later += [(name, step) for name in ("key", "value") for step in far]
    return first + later


def solution(mesh):
    count = mesh.shape["head"]
    paired = count & (count - 1) == 0

    def target(index, step):
        return index ^ step if paired else (index + step) % count

    def origin(index, step):
        return index ^ step if paired else (index - step) % count

    def per_device(queries, keys, values, text_kv, cotangent):
        here = lax.axis_index("head")
        order = jnp.stack([origin(here, step) for step in range(count)]).astype(jnp.int32)
        goal = jnp.stack([target(here, step) for step in range(count)]).astype(jnp.int32)
        arrays = {"query": queries[0], "text": text_kv[0], "key": keys[0], "value": values[0]}

        def columns(name, step):
            rows, width = arrays[name].shape
            width //= count
            at = target(here, step) * width
            return lax.dynamic_slice(arrays[name], (0, at), (rows, width))

        first, step = sends[0]
        held = pick_call(arrays[first], target(here, step), arrays[first].shape[1] // count)
        arrays[first], held = lax.optimization_barrier((arrays[first], held))
        got = {name: [columns(name, 0)] + [None] * (count - 1) for name in arrays}
        for at, (name, step) in enumerate(sends):
            got[name][step] = lax.ppermute(
                columns(name, step) if at else held,
                "head",
                [(index, target(index, step)) for index in range(count)],
            )
        cross_out, *grad_pieces = cross_call(order, got["query"], got["text"], cotangent[0])
        back = [grad_pieces[0]]
        for step in range(1, count):
            back.append(
                lax.ppermute(
                    grad_pieces[step],
                    "head",
                    [(target(index, step), index) for index in range(count)],
                )
            )
        probs = scores_call(order, got["query"], got["key"])
        attended = values_call(got["value"], probs, cross_out)
        text_grad = place_call(goal, tuple(range(count - 1)), back[:-1])
        last = back[-1]
        at = target(here, count - 1) * last.shape[1]
        text_grad = lax.dynamic_update_slice(text_grad, last, (0, at))
        return attended[None], text_grad[None]

    sends = send_order(count)

    placed = (
        P(("seq", "rep"), "head", None),
        P(("seq", "rep"), "head", None),
        P(("seq", "rep"), "head", None),
        P(("seq", "rep"), "head", None),
        P(("seq", "rep"), None, "head"),
    )
    return jax.shard_map(
        per_device,
        mesh=mesh,
        in_specs=placed,
        out_specs=(P(("seq", "rep"), None, "head"), P(("seq", "rep"), "head", None)),
        check_vma=False,
    )
```

```python
import jax
import jax.numpy as jnp
from jax import lax
from jax.experimental import pallas as pl
from jax.experimental.pallas import tpu as pltpu
from jax.sharding import PartitionSpec as P


HD = 128
GRANT = 24 << 20


def dot_nt(a, b):
    return lax.dot_general(a, b, (((1,), (1,)), ((), ())), preferred_element_type=jnp.float32)


def dot_nn(a, b):
    return lax.dot_general(a, b, (((1,), (0,)), ((), ())), preferred_element_type=jnp.float32)


def softmax_columns(scores):
    top = jnp.max(scores, axis=0, keepdims=True)
    weights = jnp.exp(scores - top)
    return weights / jnp.sum(weights, axis=0, keepdims=True)


def columns_of(ref, head, width):
    return ref[:, head * width : (head + 1) * width]


def stacked(refs, head, width):
    return jnp.concatenate([columns_of(ref, head, width) for ref in refs], axis=0)


def cross_kernel(count, origin, *refs):
    query_refs = refs[:count]
    text_refs = refs[count : 2 * count]
    grad_ref = refs[2 * count]
    out_ref = refs[2 * count + 1]
    piece_refs = refs[2 * count + 2 : 3 * count + 2]
    query_all = refs[3 * count + 2]
    scale = float(HD) ** (-0.5)
    here = lax.axis_index("head")
    rows = query_refs[0].shape[0]
    for at, ref in enumerate(query_refs):
        start = pl.multiple_of(origin(here, at) * rows, rows)
        query_all[pl.ds(start, rows), :] = ref[...]
    text_rows = text_refs[0].shape[0]
    for head in range(grad_ref.shape[1] // HD):
        query = columns_of(query_all, head, HD)
        grad = columns_of(grad_ref, head, HD)
        text = stacked(text_refs, head, 2 * HD)
        text_keys = text[:, :HD]
        text_values = text[:, HD:]
        probs = softmax_columns(dot_nt(text_keys, query) * scale)
        rounded = probs.astype(jnp.bfloat16)
        dprobs = dot_nt(text_values, grad)
        dscores = probs * (dprobs - jnp.sum(dprobs * probs, axis=0, keepdims=True))
        dscores = dscores.astype(jnp.bfloat16)
        grad_keys = (dot_nn(dscores, query) * scale).astype(jnp.bfloat16)
        grad_values = dot_nn(rounded, grad).astype(jnp.bfloat16)
        for at, ref in enumerate(piece_refs):
            part = slice(at * text_rows, (at + 1) * text_rows)
            ref[:, 2 * head * HD : (2 * head + 1) * HD] = grad_keys[part]
            ref[:, (2 * head + 1) * HD : (2 * head + 2) * HD] = grad_values[part]
        out_ref[:, head * HD : (head + 1) * HD] = dot_nn(text_values.T, rounded).T


def scores_kernel(count, origin, *refs):
    query_refs = refs[:count]
    key_refs = refs[count : 2 * count]
    probs_ref = refs[2 * count]
    scale = float(HD) ** (-0.5)
    here = lax.axis_index("head")
    rows, width = query_refs[0].shape
    length = rows * count
    for head in range(width // HD):
        keys = stacked(key_refs, head, HD)
        for at, ref in enumerate(query_refs):
            scores = dot_nt(columns_of(ref, head, HD), keys) * scale
            weights = jnp.exp(scores - jnp.max(scores, axis=1, keepdims=True))
            probs = weights / jnp.sum(weights, axis=1, keepdims=True)
            start = pl.multiple_of(origin(here, at) * rows, rows)
            probs_ref[pl.ds(start, rows), head * length : (head + 1) * length] = probs.astype(
                jnp.bfloat16
            )


def values_kernel(count, *refs):
    value_refs = refs[:count]
    probs_ref, cross_ref, out_ref = refs[count:]
    length, width = cross_ref.shape
    for head in range(width // HD):
        out = dot_nn(columns_of(probs_ref, head, length), stacked(value_refs, head, HD))
        out_ref[:, head * HD : (head + 1) * HD] = (out + columns_of(cross_ref, head, HD)).astype(
            jnp.bfloat16
        )


def vmem_call(kernel, out_shape, operands, scratch=()):
    many = isinstance(out_shape, list)
    spec = pl.BlockSpec(memory_space=pltpu.VMEM)
    return pl.pallas_call(
        kernel,
        out_shape=out_shape,
        in_specs=[spec] * len(operands),
        out_specs=[spec] * len(out_shape) if many else spec,
        scratch_shapes=list(scratch),
        compiler_params=pltpu.CompilerParams(vmem_limit_bytes=GRANT),
    )(*[pltpu.with_memory_space_constraint(operand, pltpu.VMEM) for operand in operands])


def cross_call(origin, query_pieces, text_pieces, cotangent):
    count = len(query_pieces)
    piece = pltpu.VMEM(text_pieces[0].shape, jnp.bfloat16)
    return vmem_call(
        lambda *refs: cross_kernel(count, origin, *refs),
        [pltpu.VMEM(cotangent.shape, jnp.float32)] + [piece] * count,
        [*query_pieces, *text_pieces, cotangent],
        [pltpu.VMEM(cotangent.shape, jnp.bfloat16)],
    )


def scores_call(origin, query_pieces, key_pieces):
    count = len(query_pieces)
    rows, width = query_pieces[0].shape
    length = rows * count
    return vmem_call(
        lambda *refs: scores_kernel(count, origin, *refs),
        pltpu.VMEM((length, (width // HD) * length), jnp.bfloat16),
        [*query_pieces, *key_pieces],
    )


def values_call(value_pieces, probs, cross_out):
    count = len(value_pieces)
    return vmem_call(
        lambda *refs: values_kernel(count, *refs),
        jax.ShapeDtypeStruct(cross_out.shape, jnp.bfloat16),
        [*value_pieces, probs, cross_out],
    )


def place_kernel(steps, order, *refs):
    pieces = refs[: len(steps)]
    out_ref, sems = refs[-2:]
    width = pieces[0].shape[1]
    copies = [
        pltpu.make_async_copy(
            piece,
            out_ref.at[:, pl.ds(pl.multiple_of(order[step] * width, width), width)],
            sems.at[at],
        )
        for at, (step, piece) in enumerate(zip(steps, pieces))
    ]
    for copy in copies:
        copy.start()
    for copy in copies:
        copy.wait()


def place_call(order, steps, pieces, whole=None):
    count = order.shape[0]
    rows, width = pieces[0].shape
    held = [] if whole is None else [whole]
    return pl.pallas_call(
        lambda *refs: place_kernel(steps, *refs),
        name="place",
        out_shape=jax.ShapeDtypeStruct((rows, width * count), pieces[0].dtype),
        in_specs=[pl.BlockSpec(memory_space=pltpu.SMEM)]
        + [pl.BlockSpec(memory_space=pltpu.VMEM)] * len(steps)
        + [pl.BlockSpec(memory_space=pl.ANY)] * len(held),
        out_specs=pl.BlockSpec(memory_space=pl.ANY),
        scratch_shapes=[pltpu.SemaphoreType.DMA((len(steps),))],
        input_output_aliases={len(steps) + 1: 0} if held else {},
        compiler_params=pltpu.CompilerParams(vmem_limit_bytes=GRANT),
    )(
        order,
        *[pltpu.with_memory_space_constraint(piece, pltpu.VMEM) for piece in pieces],
        *held,
    )


def pick_call(array, at, width):
    def pick_kernel(at, array_ref, out_ref, sem):
        start = pl.multiple_of(at[0] * width, width)
        copy = pltpu.make_async_copy(array_ref.at[:, pl.ds(start, width)], out_ref, sem)
        copy.start()
        copy.wait()

    return pl.pallas_call(
        pick_kernel,
        name="pick",
        out_shape=pltpu.VMEM((array.shape[0], width), array.dtype),
        in_specs=[pl.BlockSpec(memory_space=pltpu.SMEM), pl.BlockSpec(memory_space=pl.ANY)],
        out_specs=pl.BlockSpec(memory_space=pltpu.VMEM),
        scratch_shapes=[pltpu.SemaphoreType.DMA],
    )(at.reshape(1).astype(jnp.int32), array)


def send_order(count):
    near, far = [1], list(range(count - 1, 1, -1))
    first = [(name, step) for step in far[:1] for name in ("query", "text")]
    first += [(name, step) for step in near for name in ("query", "text", "key", "value")]
    later = [(name, step) for name in ("query", "text") for step in far[1:]]
    later += [(name, step) for name in ("key", "value") for step in far]
    return first + later


def solution(mesh):
    count = mesh.shape["head"]
    paired = count & (count - 1) == 0

    def target(index, step):
        return index ^ step if paired else (index + step) % count

    def origin(index, step):
        return index ^ step if paired else (index - step) % count

    def per_device(queries, keys, values, text_kv, cotangent):
        here = lax.axis_index("head")
        goal = jnp.stack([target(here, step) for step in range(count)]).astype(jnp.int32)
        arrays = {"query": queries[0], "text": text_kv[0], "key": keys[0], "value": values[0]}

        def columns(name, step):
            rows, width = arrays[name].shape
            width //= count
            at = target(here, step) * width
            return lax.dynamic_slice(arrays[name], (0, at), (rows, width))

        first, step = sends[0]
        held = pick_call(arrays[first], target(here, step), arrays[first].shape[1] // count)
        arrays[first], held = lax.optimization_barrier((arrays[first], held))
        got = {name: [columns(name, 0)] + [None] * (count - 1) for name in arrays}
        for at, (name, step) in enumerate(sends):
            got[name][step] = lax.ppermute(
                columns(name, step) if at else held,
                "head",
                [(index, target(index, step)) for index in range(count)],
            )
        cross_out, *grad_pieces = cross_call(origin, got["query"], got["text"], cotangent[0])
        back = [grad_pieces[0]]
        for step in range(1, count):
            back.append(
                lax.ppermute(
                    grad_pieces[step],
                    "head",
                    [(target(index, step), index) for index in range(count)],
                )
            )
        probs = scores_call(origin, got["query"], got["key"])
        attended = values_call(got["value"], probs, cross_out)
        text_grad = place_call(goal, tuple(range(count - 1)), back[:-1])
        last = back[-1]
        at = target(here, count - 1) * last.shape[1]
        text_grad = lax.dynamic_update_slice(text_grad, last, (0, at))
        return attended[None], text_grad[None]

    sends = send_order(count)

    placed = (
        P(("seq", "rep"), "head", None),
        P(("seq", "rep"), "head", None),
        P(("seq", "rep"), "head", None),
        P(("seq", "rep"), "head", None),
        P(("seq", "rep"), None, "head"),
    )
    return jax.shard_map(
        per_device,
        mesh=mesh,
        in_specs=placed,
        out_specs=(P(("seq", "rep"), None, "head"), P(("seq", "rep"), "head", None)),
        check_vma=False,
    )
```

```python
import jax
import jax.numpy as jnp
from jax import lax
from jax.experimental import pallas as pl
from jax.experimental.pallas import tpu as pltpu
from jax.sharding import PartitionSpec as P


HD = 128
GRANT = 24 << 20


def dot_nt(a, b):
    return lax.dot_general(a, b, (((1,), (1,)), ((), ())), preferred_element_type=jnp.float32)


def dot_nn(a, b):
    return lax.dot_general(a, b, (((1,), (0,)), ((), ())), preferred_element_type=jnp.float32)


def softmax_columns(scores):
    top = jnp.max(scores, axis=0, keepdims=True)
    weights = jnp.exp(scores - top)
    return weights / jnp.sum(weights, axis=0, keepdims=True)


def columns_of(ref, head, width):
    return ref[:, head * width : (head + 1) * width]


def stacked(refs, head, width):
    return jnp.concatenate([columns_of(ref, head, width) for ref in refs], axis=0)


def cross_kernel(count, origin, *refs):
    query_refs = refs[:count]
    text_refs = refs[count : 2 * count]
    grad_ref = refs[2 * count]
    out_ref = refs[2 * count + 1]
    piece_refs = refs[2 * count + 2 : 3 * count + 1]
    rest_ref, most_ref, query_all = refs[3 * count + 1 :]
    scale = float(HD) ** (-0.5)
    here = lax.axis_index("head")
    rows = query_refs[0].shape[0]
    for at, ref in enumerate(query_refs):
        start = pl.multiple_of(origin(here, at) * rows, rows)
        query_all[pl.ds(start, rows), :] = ref[...]
    text_rows = text_refs[0].shape[0]
    for head in range(grad_ref.shape[1] // HD):
        query = columns_of(query_all, head, HD)
        grad = columns_of(grad_ref, head, HD)
        text = stacked(text_refs, head, 2 * HD)
        text_keys = text[:, :HD]
        text_values = text[:, HD:]
        probs = softmax_columns(dot_nt(text_keys, query) * scale)
        rounded = probs.astype(jnp.bfloat16)
        dprobs = dot_nt(text_values, grad)
        dscores = probs * (dprobs - jnp.sum(dprobs * probs, axis=0, keepdims=True))
        dscores = dscores.astype(jnp.bfloat16)
        grad_keys = (dot_nn(dscores, query) * scale).astype(jnp.bfloat16)
        grad_values = dot_nn(rounded, grad).astype(jnp.bfloat16)
        places = [(ref, 2 * head * HD) for ref in piece_refs]
        few = rest_ref.shape[1] // (2 * HD)
        places.append(
            (rest_ref, 2 * head * HD) if head < few else (most_ref, 2 * (head - few) * HD)
        )
        for at, (ref, start) in enumerate(places):
            part = slice(at * text_rows, (at + 1) * text_rows)
            ref[:, start : start + HD] = grad_keys[part]
            ref[:, start + HD : start + 2 * HD] = grad_values[part]
        out_ref[:, head * HD : (head + 1) * HD] = dot_nn(text_values.T, rounded).T


def scores_kernel(count, origin, *refs):
    query_refs = refs[:count]
    key_refs = refs[count : 2 * count]
    probs_ref = refs[2 * count]
    scale = float(HD) ** (-0.5)
    here = lax.axis_index("head")
    rows, width = query_refs[0].shape
    length = rows * count
    for head in range(width // HD):
        keys = stacked(key_refs, head, HD)
        for at, ref in enumerate(query_refs):
            scores = dot_nt(columns_of(ref, head, HD), keys) * scale
            weights = jnp.exp(scores - jnp.max(scores, axis=1, keepdims=True))
            probs = weights / jnp.sum(weights, axis=1, keepdims=True)
            start = pl.multiple_of(origin(here, at) * rows, rows)
            probs_ref[pl.ds(start, rows), head * length : (head + 1) * length] = probs.astype(
                jnp.bfloat16
            )


def values_kernel(count, *refs):
    value_refs = refs[:count]
    probs_ref, cross_ref, out_ref = refs[count:]
    length, width = cross_ref.shape
    for head in range(width // HD):
        out = dot_nn(columns_of(probs_ref, head, length), stacked(value_refs, head, HD))
        out_ref[:, head * HD : (head + 1) * HD] = (out + columns_of(cross_ref, head, HD)).astype(
            jnp.bfloat16
        )


def vmem_call(kernel, out_shape, operands, scratch=()):
    many = isinstance(out_shape, list)
    spec = pl.BlockSpec(memory_space=pltpu.VMEM)
    return pl.pallas_call(
        kernel,
        out_shape=out_shape,
        in_specs=[spec] * len(operands),
        out_specs=[spec] * len(out_shape) if many else spec,
        scratch_shapes=list(scratch),
        compiler_params=pltpu.CompilerParams(vmem_limit_bytes=GRANT),
    )(*[pltpu.with_memory_space_constraint(operand, pltpu.VMEM) for operand in operands])


def cross_call(origin, query_pieces, text_pieces, cotangent):
    count = len(query_pieces)
    rows, width = text_pieces[0].shape
    pieces = [pltpu.VMEM((rows, width), jnp.bfloat16)] * (count - 1)
    pieces += [pltpu.VMEM((rows, wide), jnp.bfloat16) for wide in (width // 2, width // 2)]
    return vmem_call(
        lambda *refs: cross_kernel(count, origin, *refs),
        [pltpu.VMEM(cotangent.shape, jnp.float32)] + pieces,
        [*query_pieces, *text_pieces, cotangent],
        [pltpu.VMEM(cotangent.shape, jnp.bfloat16)],
    )


def scores_call(origin, query_pieces, key_pieces):
    count = len(query_pieces)
    rows, width = query_pieces[0].shape
    length = rows * count
    return vmem_call(
        lambda *refs: scores_kernel(count, origin, *refs),
        pltpu.VMEM((length, (width // HD) * length), jnp.bfloat16),
        [*query_pieces, *key_pieces],
    )


def values_call(value_pieces, probs, cross_out):
    count = len(value_pieces)
    return vmem_call(
        lambda *refs: values_kernel(count, *refs),
        jax.ShapeDtypeStruct(cross_out.shape, jnp.bfloat16),
        [*value_pieces, probs, cross_out],
    )


def place_kernel(steps, order, *refs):
    pieces = refs[: len(steps)]
    out_ref, sems = refs[-2:]
    width = pieces[0].shape[1]
    copies = []
    for at, (step, piece) in enumerate(zip(steps, pieces)):
        start = pl.multiple_of(order[step] * width, width) + width - piece.shape[1]
        spot = out_ref.at[:, pl.ds(pl.multiple_of(start, HD), piece.shape[1])]
        copies.append(pltpu.make_async_copy(piece, spot, sems.at[at]))
    for copy in copies:
        copy.start()
    for copy in copies:
        copy.wait()


def place_call(order, steps, pieces, whole=None):
    count = order.shape[0]
    rows, width = pieces[0].shape
    held = [] if whole is None else [whole]
    return pl.pallas_call(
        lambda *refs: place_kernel(steps, *refs),
        name="place",
        out_shape=jax.ShapeDtypeStruct((rows, width * count), pieces[0].dtype),
        in_specs=[pl.BlockSpec(memory_space=pltpu.SMEM)]
        + [pl.BlockSpec(memory_space=pltpu.VMEM)] * len(steps)
        + [pl.BlockSpec(memory_space=pl.ANY)] * len(held),
        out_specs=pl.BlockSpec(memory_space=pl.ANY),
        scratch_shapes=[pltpu.SemaphoreType.DMA((len(steps),))],
        input_output_aliases={len(steps) + 1: 0} if held else {},
        compiler_params=pltpu.CompilerParams(vmem_limit_bytes=GRANT),
    )(
        order,
        *[pltpu.with_memory_space_constraint(piece, pltpu.VMEM) for piece in pieces],
        *held,
    )


def pick_call(array, at, width):
    def pick_kernel(at, array_ref, out_ref, sem):
        start = pl.multiple_of(at[0] * width, width)
        copy = pltpu.make_async_copy(array_ref.at[:, pl.ds(start, width)], out_ref, sem)
        copy.start()
        copy.wait()

    return pl.pallas_call(
        pick_kernel,
        name="pick",
        out_shape=pltpu.VMEM((array.shape[0], width), array.dtype),
        in_specs=[pl.BlockSpec(memory_space=pltpu.SMEM), pl.BlockSpec(memory_space=pl.ANY)],
        out_specs=pl.BlockSpec(memory_space=pltpu.VMEM),
        scratch_shapes=[pltpu.SemaphoreType.DMA],
    )(at.reshape(1).astype(jnp.int32), array)


def send_order(count):
    near, far = [1], list(range(count - 1, 1, -1))
    first = [(name, step) for step in far[:1] for name in ("query", "text")]
    first += [(name, step) for step in near for name in ("query", "text", "key", "value")]
    later = [(name, step) for name in ("query", "text") for step in far[1:]]
    later += [(name, step) for name in ("key", "value") for step in far]
    return first + later


def solution(mesh):
    count = mesh.shape["head"]
    paired = count & (count - 1) == 0

    def target(index, step):
        return index ^ step if paired else (index + step) % count

    def origin(index, step):
        return index ^ step if paired else (index - step) % count

    def per_device(queries, keys, values, text_kv, cotangent):
        here = lax.axis_index("head")
        goal = jnp.stack([target(here, step) for step in range(count)]).astype(jnp.int32)
        arrays = {"query": queries[0], "text": text_kv[0], "key": keys[0], "value": values[0]}

        def columns(name, step):
            rows, width = arrays[name].shape
            width //= count
            at = target(here, step) * width
            return lax.dynamic_slice(arrays[name], (0, at), (rows, width))

        first, step = sends[0]
        held = pick_call(arrays[first], target(here, step), arrays[first].shape[1] // count)
        arrays[first], held = lax.optimization_barrier((arrays[first], held))
        got = {name: [columns(name, 0)] + [None] * (count - 1) for name in arrays}
        for at, (name, step) in enumerate(sends):
            got[name][step] = lax.ppermute(
                columns(name, step) if at else held,
                "head",
                [(index, target(index, step)) for index in range(count)],
            )
        cross_out, *grad_pieces = cross_call(origin, got["query"], got["text"], cotangent[0])

        def send_back(piece, step):
            return lax.ppermute(
                piece, "head", [(target(index, step), index) for index in range(count)]
            )

        back = [grad_pieces[0]]
        for step in range(1, count - 1):
            back.append(send_back(grad_pieces[step], step))
        most = send_back(grad_pieces[count], count - 1)
        rest = send_back(grad_pieces[count - 1], count - 1)
        probs = scores_call(origin, got["query"], got["key"])
        attended = values_call(got["value"], probs, cross_out)
        text_grad = place_call(goal, tuple(range(count)), back + [most])
        at = target(here, count - 1) * grad_pieces[0].shape[1]
        text_grad = lax.dynamic_update_slice(text_grad, rest, (0, at))
        return attended[None], text_grad[None]

    sends = send_order(count)

    placed = (
        P(("seq", "rep"), "head", None),
        P(("seq", "rep"), "head", None),
        P(("seq", "rep"), "head", None),
        P(("seq", "rep"), "head", None),
        P(("seq", "rep"), None, "head"),
    )
    return jax.shard_map(
        per_device,
        mesh=mesh,
        in_specs=placed,
        out_specs=(P(("seq", "rep"), None, "head"), P(("seq", "rep"), "head", None)),
        check_vma=False,
    )
```

```python
import jax
import jax.numpy as jnp
from jax import lax
from jax.experimental import pallas as pl
from jax.experimental.pallas import tpu as pltpu
from jax.sharding import PartitionSpec as P


HD = 128
GRANT = 24 << 20


def dot_nt(a, b):
    return lax.dot_general(a, b, (((1,), (1,)), ((), ())), preferred_element_type=jnp.float32)


def dot_nn(a, b):
    return lax.dot_general(a, b, (((1,), (0,)), ((), ())), preferred_element_type=jnp.float32)


def softmax_columns(scores):
    top = jnp.max(scores, axis=0, keepdims=True)
    weights = jnp.exp(scores - top)
    return weights / jnp.sum(weights, axis=0, keepdims=True)


def columns_of(ref, head, width):
    return ref[:, head * width : (head + 1) * width]


def stacked(refs, head, width):
    return jnp.concatenate([columns_of(ref, head, width) for ref in refs], axis=0)


def cross_kernel(count, origin, *refs):
    query_refs = refs[:count]
    text_refs = refs[count : 2 * count]
    grad_ref = refs[2 * count]
    out_ref = refs[2 * count + 1]
    piece_refs = refs[2 * count + 2 : 3 * count + 2]
    query_all = refs[3 * count + 2]
    scale = float(HD) ** (-0.5)
    here = lax.axis_index("head")
    rows = query_refs[0].shape[0]
    for at, ref in enumerate(query_refs):
        start = pl.multiple_of(origin(here, at) * rows, rows)
        query_all[pl.ds(start, rows), :] = ref[...]
    text_rows = text_refs[0].shape[0]
    for head in range(grad_ref.shape[1] // HD):
        query = columns_of(query_all, head, HD)
        grad = columns_of(grad_ref, head, HD)
        text = stacked(text_refs, head, 2 * HD)
        text_keys = text[:, :HD]
        text_values = text[:, HD:]
        probs = softmax_columns(dot_nt(text_keys, query) * scale)
        rounded = probs.astype(jnp.bfloat16)
        dprobs = dot_nt(text_values, grad)
        dscores = probs * (dprobs - jnp.sum(dprobs * probs, axis=0, keepdims=True))
        dscores = dscores.astype(jnp.bfloat16)
        grad_keys = (dot_nn(dscores, query) * scale).astype(jnp.bfloat16)
        grad_values = dot_nn(rounded, grad).astype(jnp.bfloat16)
        for at, ref in enumerate(piece_refs):
            part = slice(at * text_rows, (at + 1) * text_rows)
            ref[:, 2 * head * HD : (2 * head + 1) * HD] = grad_keys[part]
            ref[:, (2 * head + 1) * HD : (2 * head + 2) * HD] = grad_values[part]
        out_ref[:, head * HD : (head + 1) * HD] = dot_nn(text_values.T, rounded).T


def scores_kernel(count, origin, *refs):
    query_refs = refs[:count]
    key_refs = refs[count : 2 * count]
    probs_ref = refs[2 * count]
    scale = float(HD) ** (-0.5)
    here = lax.axis_index("head")
    rows, width = query_refs[0].shape
    length = rows * count
    for head in range(width // HD):
        keys = stacked(key_refs, head, HD)
        for at, ref in enumerate(query_refs):
            scores = dot_nt(columns_of(ref, head, HD), keys) * scale
            weights = jnp.exp(scores - jnp.max(scores, axis=1, keepdims=True))
            probs = weights / jnp.sum(weights, axis=1, keepdims=True)
            start = pl.multiple_of(origin(here, at) * rows, rows)
            probs_ref[pl.ds(start, rows), head * length : (head + 1) * length] = probs.astype(
                jnp.bfloat16
            )


def values_kernel(count, *refs):
    value_refs = refs[:count]
    probs_ref, cross_ref, out_ref = refs[count:]
    length, width = cross_ref.shape
    for head in range(width // HD):
        out = dot_nn(columns_of(probs_ref, head, length), stacked(value_refs, head, HD))
        out_ref[:, head * HD : (head + 1) * HD] = (out + columns_of(cross_ref, head, HD)).astype(
            jnp.bfloat16
        )


def vmem_call(kernel, out_shape, operands, scratch=()):
    many = isinstance(out_shape, list)
    spec = pl.BlockSpec(memory_space=pltpu.VMEM)
    return pl.pallas_call(
        kernel,
        out_shape=out_shape,
        in_specs=[spec] * len(operands),
        out_specs=[spec] * len(out_shape) if many else spec,
        scratch_shapes=list(scratch),
        compiler_params=pltpu.CompilerParams(vmem_limit_bytes=GRANT),
    )(*[pltpu.with_memory_space_constraint(operand, pltpu.VMEM) for operand in operands])


def cross_call(origin, query_pieces, text_pieces, cotangent):
    count = len(query_pieces)
    piece = pltpu.VMEM(text_pieces[0].shape, jnp.bfloat16)
    return vmem_call(
        lambda *refs: cross_kernel(count, origin, *refs),
        [pltpu.VMEM(cotangent.shape, jnp.float32)] + [piece] * count,
        [*query_pieces, *text_pieces, cotangent],
        [pltpu.VMEM(cotangent.shape, jnp.bfloat16)],
    )


def scores_call(origin, query_pieces, key_pieces):
    count = len(query_pieces)
    rows, width = query_pieces[0].shape
    length = rows * count
    return vmem_call(
        lambda *refs: scores_kernel(count, origin, *refs),
        pltpu.VMEM((length, (width // HD) * length), jnp.bfloat16),
        [*query_pieces, *key_pieces],
    )


def values_call(value_pieces, probs, cross_out):
    count = len(value_pieces)
    return vmem_call(
        lambda *refs: values_kernel(count, *refs),
        jax.ShapeDtypeStruct(cross_out.shape, jnp.bfloat16),
        [*value_pieces, probs, cross_out],
    )


def place_kernel(steps, order, *refs):
    pieces = refs[: len(steps)]
    out_ref, sems = refs[-2:]
    width = pieces[0].shape[1]
    copies = [
        pltpu.make_async_copy(
            piece,
            out_ref.at[:, pl.ds(pl.multiple_of(order[step] * width, width), width)],
            sems.at[at],
        )
        for at, (step, piece) in enumerate(zip(steps, pieces))
    ]
    for copy in copies:
        copy.start()
    for copy in copies:
        copy.wait()


def place_call(order, steps, pieces, whole=None):
    count = order.shape[0]
    rows, width = pieces[0].shape
    held = [] if whole is None else [whole]
    return pl.pallas_call(
        lambda *refs: place_kernel(steps, *refs),
        name="place",
        out_shape=jax.ShapeDtypeStruct((rows, width * count), pieces[0].dtype),
        in_specs=[pl.BlockSpec(memory_space=pltpu.SMEM)]
        + [pl.BlockSpec(memory_space=pltpu.VMEM)] * len(steps)
        + [pl.BlockSpec(memory_space=pl.ANY)] * len(held),
        out_specs=pl.BlockSpec(memory_space=pl.ANY),
        scratch_shapes=[pltpu.SemaphoreType.DMA((len(steps),))],
        input_output_aliases={len(steps) + 1: 0} if held else {},
        compiler_params=pltpu.CompilerParams(vmem_limit_bytes=GRANT),
    )(
        order,
        *[pltpu.with_memory_space_constraint(piece, pltpu.VMEM) for piece in pieces],
        *held,
    )


def pick_call(array, at, width):
    def pick_kernel(at, array_ref, out_ref, sem):
        start = pl.multiple_of(at[0] * width, width)
        copy = pltpu.make_async_copy(array_ref.at[:, pl.ds(start, width)], out_ref, sem)
        copy.start()
        copy.wait()

    return pl.pallas_call(
        pick_kernel,
        name="pick",
        out_shape=pltpu.VMEM((array.shape[0], width), array.dtype),
        in_specs=[pl.BlockSpec(memory_space=pltpu.SMEM), pl.BlockSpec(memory_space=pl.ANY)],
        out_specs=pl.BlockSpec(memory_space=pltpu.VMEM),
        scratch_shapes=[pltpu.SemaphoreType.DMA],
    )(at.reshape(1).astype(jnp.int32), array)


def send_order(count):
    steps = range(count - 1, 0, -1)
    return [
        (name, step)
        for names in (("query", "text"), ("key", "value"))
        for step in steps
        for name in names
    ]


def solution(mesh):
    count = mesh.shape["head"]
    paired = count & (count - 1) == 0

    def target(index, step):
        return index ^ step if paired else (index + step) % count

    def origin(index, step):
        return index ^ step if paired else (index - step) % count

    def per_device(queries, keys, values, text_kv, cotangent):
        here = lax.axis_index("head")
        goal = jnp.stack([target(here, step) for step in range(count)]).astype(jnp.int32)
        arrays = {"query": queries[0], "text": text_kv[0], "key": keys[0], "value": values[0]}

        def columns(name, step):
            rows, width = arrays[name].shape
            width //= count
            at = target(here, step) * width
            return lax.dynamic_slice(arrays[name], (0, at), (rows, width))

        first, step = sends[0]
        held = pick_call(arrays[first], target(here, step), arrays[first].shape[1] // count)
        arrays[first], held = lax.optimization_barrier((arrays[first], held))
        got = {name: [columns(name, 0)] + [None] * (count - 1) for name in arrays}
        for at, (name, step) in enumerate(sends):
            got[name][step] = lax.ppermute(
                columns(name, step) if at else held,
                "head",
                [(index, target(index, step)) for index in range(count)],
            )
        cross_out, *grad_pieces = cross_call(origin, got["query"], got["text"], cotangent[0])
        back = [grad_pieces[0]]
        for step in range(1, count):
            back.append(
                lax.ppermute(
                    grad_pieces[step],
                    "head",
                    [(target(index, step), index) for index in range(count)],
                )
            )
        probs = scores_call(origin, got["query"], got["key"])
        attended = values_call(got["value"], probs, cross_out)
        text_grad = place_call(goal, tuple(range(count - 1)), back[:-1])
        last = back[-1]
        at = target(here, count - 1) * last.shape[1]
        text_grad = lax.dynamic_update_slice(text_grad, last, (0, at))
        return attended[None], text_grad[None]

    sends = send_order(count)

    placed = (
        P(("seq", "rep"), "head", None),
        P(("seq", "rep"), "head", None),
        P(("seq", "rep"), "head", None),
        P(("seq", "rep"), "head", None),
        P(("seq", "rep"), None, "head"),
    )
    return jax.shard_map(
        per_device,
        mesh=mesh,
        in_specs=placed,
        out_specs=(P(("seq", "rep"), None, "head"), P(("seq", "rep"), "head", None)),
        check_vma=False,
    )
```
